32 devices in a mesh: snap: 4 (over z), vert: 8 (over y, x, core).
Axes of the slice: x: 2, y: 2, z: 4, core: 2. Of those that a mesh axis runs over, the one named last changes fastest.
Arguments:
- features: bfloat16 [8, 16384, 256], P('snap', 'vert'), may hold values from -6 to 6
- tile_rows: int32 [8, 512], P('snap', 'vert'), may hold values from 0 to 15
- tile_cols: int32 [8, 512], P('snap', 'vert'), may hold values from 0 to 21
- tile_vals: bfloat16 [8, 512, 128, 128], P('snap', 'vert'), may hold values from -0.25 to 0.25
- send_lists: int32 [8, 6], replicated, may hold values from 0 to 15
- conv1_weight: bfloat16 [256, 256], replicated, may hold values from -0.375 to 0.375
- conv2_weight: bfloat16 [256, 256], replicated, may hold values from -0.375 to 0.375
- lstm_weight: bfloat16 [2, 512, 1024], replicated, may hold values from -0.25 to 0.25
- lstm_bias: float32 [2, 1024], replicated, may hold values from -4 to 4
Outputs:
- mixed: bfloat16 [8, 16384, 256], P('snap', 'vert')
The draws below stay inside these ranges and needn't reach their ends.
All inputs are finite; a program needn't handle non-finite values.
Results may differ from the reference program's by a relative error of at most 0.007.
Values may be sent and summed in bfloat16 or wider, within the bound.
No kernel may reach another device: no remote copies, remote signals or barrier semaphores. Data moves between devices by JAX's collectives and lax.ppermute only.
A program may use at most 128 MiB of HBM per device.

```python
import jax
import jax.numpy as jnp
from jax import lax

F = 256
BS = 128
BND = 3
BLK_DEV = 16
TILE_DEV = 64
SNAPS = 8
VERTS = 16384
TILES = 512
N_VERT = 8


def plant(drawn, stream_key, smallest, high):
    shape = drawn.shape
    place = [jax.random.randint(jax.random.fold_in(stream_key, axis), (), 0, shape[axis]) for axis in range(len(shape))]
    drawn = drawn.at[tuple(place)].set(smallest)
    longest = shape.index(max(shape))
    place[longest] = (place[longest] + 1) % shape[longest]
    return drawn.at[tuple(place)].set(high)


def block_scale(stream_key, shape, shards, smallest, top_value):
    def one(dim, shards_of):
        heights = jax.random.uniform(jax.random.fold_in(jax.random.fold_in(stream_key, 6), dim), (shards_of,), jnp.float32, smallest / len(shards), top_value / len(shards))
        return jnp.repeat(jnp.exp(heights), shape[dim] // shards_of).reshape((-1,) + (1,) * (len(shape) - dim - 1))

    gain = one(*shards[0])
    for cut in shards[1:]:
        gain = gain * one(*cut)
    return gain


def gaussian(rng, dims, width, bound, cuts=(), kind=jnp.bfloat16):
    array = jax.random.normal(rng, dims, jnp.float32) * width
    if len(cuts) > 0:
        array = block_scale(rng, dims, cuts, -0.22, 0.18) * array
    return jnp.clip(array, min=-bound, max=bound).astype(kind)


def setup_inputs(seed: int = 0) -> dict:
    key_list = jax.random.split(jax.random.key(seed), 10)
    features = gaussian(key_list[0], (SNAPS, VERTS, F), 1.0, 6.0, ((0, 4), (1, 8)))
    tile_rows = plant(jax.random.randint(key_list[1], (SNAPS, TILES), 0, BLK_DEV), jax.random.fold_in(key_list[1], 1), 0, BLK_DEV - 1).astype(jnp.int32)
    tile_cols = plant(jax.random.randint(key_list[2], (SNAPS, TILES), 0, BLK_DEV + 2 * BND), jax.random.fold_in(key_list[2], 1), 0, (BLK_DEV + 2 * BND) - 1).astype(jnp.int32)
    tile_vals = gaussian(key_list[3], (SNAPS, TILES, BS, BS), (BS * max(TILE_DEV // BLK_DEV, 1)) ** -0.5, 0.25, ((0, 4), (1, 8)))
    send_lists = plant(jax.random.randint(key_list[4], (N_VERT, 2 * BND), 0, BLK_DEV), jax.random.fold_in(key_list[4], 1), 0, BLK_DEV - 1).astype(jnp.int32)
    conv1_weight = gaussian(key_list[5], (F, F), F ** -0.5, 0.375)
    conv2_weight = gaussian(key_list[6], (F, F), F ** -0.5, 0.375)
    lstm_weight = gaussian(key_list[7], (2, 2 * F, 4 * F), (2 * F) ** -0.5, 0.25)
    lstm_bias = gaussian(key_list[8], (2, 4 * F), 1.0, 4.0, (), jnp.float32)
    return {"features": features, "tile_rows": tile_rows, "tile_cols": tile_cols, "tile_vals": tile_vals, "send_lists": send_lists, "conv1_weight": conv1_weight, "conv2_weight": conv2_weight, "lstm_weight": lstm_weight, "lstm_bias": lstm_bias}


def convolve(field, tile_rows, tile_cols, tile_vals, send_lists):
    left_list = jnp.roll(send_lists, 1, axis=0)[:, BND:].astype(jnp.int32)
    right_list = jnp.roll(send_lists, -1, axis=0)[:, :BND].astype(jnp.int32)

    def single(packed):
        slab, rows_t, cols_t, vals_t = packed
        blocks = slab.reshape(N_VERT, BLK_DEV, BS, F)
        left = jnp.take_along_axis(jnp.roll(blocks, 1, axis=0), left_list[:, :, None, None], axis=1)
        right = jnp.take_along_axis(jnp.roll(blocks, -1, axis=0), right_list[:, :, None, None], axis=1)
        extended = jnp.concatenate([left, blocks, right], axis=1)
        picked = jnp.take_along_axis(extended, cols_t.reshape(N_VERT, TILE_DEV)[:, :, None, None].astype(jnp.int32), axis=1)
        values = vals_t.reshape(N_VERT, TILE_DEV, BS, BS)
        product = jnp.einsum("dkij,dkjf->dkif", values.astype(jnp.float32), picked.astype(jnp.float32), precision=lax.Precision.HIGHEST)
        onehot = (rows_t.reshape(N_VERT, TILE_DEV)[:, :, None] == jnp.arange(BLK_DEV, dtype=jnp.int32)).astype(jnp.float32)
        summed = jnp.einsum("dkb,dkif->dbif", onehot, product, precision=lax.Precision.HIGHEST)
        return summed.reshape(N_VERT * BLK_DEV * BS, F)

    return lax.map(single, (field, tile_rows, tile_cols, tile_vals))


def project(field, weight):
    return jnp.einsum("svf,fg->svg", field.astype(jnp.float32), weight.astype(jnp.float32), precision=lax.Precision.HIGHEST).astype(jnp.bfloat16)


def cell_step(inputs, hidden, memory, weight, bias):
    gates = jnp.dot(jnp.concatenate([inputs, hidden], axis=-1), weight, preferred_element_type=jnp.float32) + bias
    in_gate, forget, candidate, out_gate = jnp.split(gates, 4, axis=-1)
    memory = jax.nn.sigmoid(forget) * memory + jax.nn.sigmoid(in_gate) * jnp.tanh(candidate)
    hidden = (jax.nn.sigmoid(out_gate) * jnp.tanh(memory)).astype(jnp.bfloat16)
    return hidden, memory


def recurrence(sequence, lstm_weight, lstm_bias):
    count = sequence.shape[1]
    zero_h = jnp.zeros((count, F), jnp.bfloat16)
    zero_c = jnp.zeros((count, F), jnp.float32)

    def advance(carry, inputs):
        first_h, first_c, second_h, second_c = carry
        first_h, first_c = cell_step(inputs, first_h, first_c, lstm_weight[0], lstm_bias[0])
        second_h, second_c = cell_step(first_h, second_h, second_c, lstm_weight[1], lstm_bias[1])
        return (first_h, first_c, second_h, second_c), second_h

    carry, outputs = lax.scan(advance, (zero_h, zero_c, zero_h, zero_c), sequence)
    return outputs


def reference(features, tile_rows, tile_cols, tile_vals, send_lists, conv1_weight, conv2_weight, lstm_weight, lstm_bias):
    projected = project(features, conv1_weight)
    convolved = jnp.maximum(convolve(projected, tile_rows, tile_cols, tile_vals, send_lists), 0.0).astype(jnp.bfloat16)
    recurrent = recurrence(convolved, lstm_weight, lstm_bias)
    second = project(recurrent, conv2_weight)
    return convolve(second, tile_rows, tile_cols, tile_vals, send_lists).astype(jnp.bfloat16)
```

```python
import functools

import jax
import jax.numpy as jnp
from jax import lax
from jax.experimental import pallas as pl
from jax.experimental.pallas import tpu as pltpu
from jax.sharding import PartitionSpec as P

BS = 128
ANY = pl.BlockSpec(memory_space=pl.ANY)
VMEM = pl.BlockSpec(memory_space=pltpu.VMEM)
SMEM = pl.BlockSpec(memory_space=pltpu.SMEM)
BF16 = jnp.bfloat16
F32 = jnp.float32


def at_snapshot(snapshot, shape):
    zeros = (0,) * len(shape)
    return pl.BlockSpec((None,) + shape, lambda i: (snapshot,) + zeros)


def whole(shape):
    zeros = (0,) * len(shape)
    return pl.BlockSpec(shape, lambda i: zeros)


def params(mib):
    return pltpu.CompilerParams(vmem_limit_bytes=mib << 20)


def pick_kernel(snapshots, bound, lists, field, *refs):
    outs, sem = refs[:-1], refs[-1]
    copies = []
    for snapshot in range(snapshots):
        for entry in range(2 * bound):
            side, slot = divmod(entry, bound)
            source = pl.multiple_of(lists[entry] * BS, BS)
            copies.append(
                pltpu.make_async_copy(
                    field.at[snapshot, pl.ds(source, BS)],
                    outs[2 * snapshot + side].at[pl.ds(slot * BS, BS)],
                    sem.at[snapshot, entry],
                )
            )
    for copy in copies:
        copy.start()
    for copy in copies:
        copy.wait()


def pick(features, own_list):
    snapshots, _, width = features.shape
    bound = own_list.shape[0] // 2
    side = jax.ShapeDtypeStruct((bound * BS, width), features.dtype)
    return pl.pallas_call(
        functools.partial(pick_kernel, snapshots, bound),
        out_shape=[side] * (2 * snapshots),
        in_specs=[SMEM, ANY],
        out_specs=[VMEM] * (2 * snapshots),
        scratch_shapes=[pltpu.SemaphoreType.DMA((snapshots, 2 * bound))],
        name="pick",
    )(own_list, features)


def add_tiles(snapshot, rows, cols, vals, vals_sem, buffer, extended, total, parts):
    tiles = buffer.shape[0]
    each = tiles // parts
    total[...] = jnp.zeros_like(total)
    for part in range(parts):
        pltpu.make_async_copy(
            vals.at[snapshot, pl.ds(part * each, each)],
            buffer.at[pl.ds(part * each, each)],
            vals_sem.at[part],
        ).wait()
        group = 8 if each % 8 == 0 else 1

        def body(step, carry):
            for inner in range(group):
                tile = part * each + step * group + inner
                row = pl.multiple_of(rows[snapshot, tile] * BS, BS)
                col = pl.multiple_of(cols[snapshot, tile] * BS, BS)
                total[pl.ds(row, BS), :] += jnp.dot(
                    buffer[tile], extended[pl.ds(col, BS), :], preferred_element_type=F32
                )
            return carry

        lax.fori_loop(0, each // group, body, 0)


def start_tiles(snapshot, vals, vals_sem, buffer, parts):
    each = buffer.shape[0] // parts
    for part in range(parts):
        pltpu.make_async_copy(
            vals.at[snapshot, pl.ds(part * each, each)],
            buffer.at[pl.ds(part * each, each)],
            vals_sem.at[part],
        ).start()


def project_into(source, weight, target, base):
    count = source.shape[0]
    step = min(256, count)
    if count % step:
        step = BS

    def body(index, carry):
        start = pl.multiple_of(index * step, step)
        target[pl.ds(pl.multiple_of(base + index * step, BS), step), :] = jnp.dot(
            source[pl.ds(start, step), :], weight[...], preferred_element_type=F32
        ).astype(BF16)
        return carry

    lax.fori_loop(0, count // step, body, 0)


def first_kernel(snapshot, groups, parts, places, rows, cols, field, low, high, weight, vals, *refs):
    aliased = groups if snapshot else 0
    outs = refs[aliased : aliased + 2 * groups]
    buffer, extended, total, sem = refs[aliased + 2 * groups :]
    start_tiles(snapshot, vals, sem, buffer, parts)
    side = low.shape[0]
    own = field.shape[0]
    project_into(field, weight, extended, side)
    project_into(low, weight, extended, 0)
    project_into(high, weight, extended, side + own)
    add_tiles(snapshot, rows, cols, vals, sem, buffer, extended, total, parts)
    share = own // groups
    half = share // 2
    for peer in range(groups):
        base = places[0, peer] * share
        for chunk in range(2):
            start = pl.multiple_of(base + chunk * half, half)
            outs[2 * peer + chunk][...] = jnp.maximum(total[pl.ds(start, half), :], 0.0).astype(BF16)


def first(snapshot, places, rows, cols, features, low, high, weight, vals, before):
    snapshots, own, width = features.shape
    tiles = vals.shape[1]
    groups = places.shape[1]
    half = own // groups // 2
    side = low.shape[0]
    parts = 4 if tiles % 4 == 0 else 1
    single = jax.ShapeDtypeStruct((half, width), BF16)
    double = jax.ShapeDtypeStruct((snapshots, half, width), BF16)
    outs, specs, aliases = [], [], {}
    for peer in range(groups):
        outs += [single, double]
        specs += [whole((half, width)), at_snapshot(snapshot, (half, width))]
        if before:
            aliases[8 + peer] = 2 * peer + 1
    return pl.pallas_call(
        functools.partial(first_kernel, snapshot, groups, parts),
        grid=(1,),
        out_shape=outs,
        in_specs=[SMEM, SMEM, SMEM, at_snapshot(snapshot, (own, width)), whole((side, width)),
                  whole((side, width)), whole((width, width)), ANY] + [ANY] * len(before),
        out_specs=specs,
        scratch_shapes=[
            pltpu.VMEM((tiles, BS, BS), BF16),
            pltpu.VMEM((own + 2 * side, width), BF16),
            pltpu.VMEM((own, width), F32),
            pltpu.SemaphoreType.DMA((parts,)),
        ],
        input_output_aliases=aliases,
        compiler_params=params(32),
        name="first",
    )(places, rows, cols, features, low, high, weight, vals, *before)


def sigmoid(value):
    return 0.5 * jnp.tanh(0.5 * value) + 0.5


def gate_cell(gates, cell, width):
    keep = sigmoid(gates[:, width : 2 * width]) * cell
    cell = keep + sigmoid(gates[:, :width]) * jnp.tanh(gates[:, 2 * width : 3 * width])
    hidden = (sigmoid(gates[:, 3 * width :]) * jnp.tanh(cell)).astype(BF16)
    return hidden, cell


def lstm_kernel(groups, snapshots, stacked_in, stacked_out, places, *refs):
    ins = refs[: groups if stacked_in else groups * snapshots]
    refs = refs[len(ins) :]
    weight, bias = refs[:2]
    refs = refs[2:]
    outs = refs[: groups if stacked_out else groups * snapshots]
    sequence, hidden0, cell0, hidden1, cell1 = refs[len(outs) :]
    steps, count, width = sequence.shape
    for peer in range(groups):
        for snapshot in range(snapshots):
            step = places[1, peer] * snapshots + snapshot
            if stacked_in:
                sequence[step] = ins[peer][snapshot]
            else:
                sequence[step] = ins[peer * snapshots + snapshot][...]

    def gates(layer, inputs, hidden):
        return (
            jnp.dot(inputs, weight[layer, :width, :], preferred_element_type=F32)
            + jnp.dot(hidden, weight[layer, width:, :], preferred_element_type=F32)
            + bias[layer : layer + 1, :]
        )

    part = min(count, BS)
    pieces = [pl.ds(start, part) for start in range(0, count, part)]

    def layer0(step):
        for piece in pieces:
            hidden, cell = gate_cell(
                gates(0, sequence[step, piece], hidden0[piece]), cell0[piece], width
            )
            hidden0[piece] = hidden
            cell0[piece] = cell

    for ref in (hidden0, cell0, hidden1, cell1):
        ref[...] = jnp.zeros_like(ref)
    layer0(0)

    def both(step, carry):
        for piece in pieces:
            shared = hidden0[piece]
            gates0 = gates(0, sequence[step + 1, piece], shared)
            gates1 = gates(1, shared, hidden1[piece])
            hidden, cell = gate_cell(gates0, cell0[piece], width)
            hidden0[piece] = hidden
            cell0[piece] = cell
            hidden, cell = gate_cell(gates1, cell1[piece], width)
            hidden1[piece] = hidden
            cell1[piece] = cell
            sequence[step, piece] = hidden
        return carry

    lax.fori_loop(0, steps - 1, both, 0)
    for piece in pieces:
        hidden, cell = gate_cell(gates(1, hidden0[piece], hidden1[piece]), cell1[piece], width)
        sequence[steps - 1, piece] = hidden
    for peer in range(groups):
        for snapshot in range(snapshots):
            step = places[0, peer] * snapshots + snapshot
            if stacked_out:
                outs[peer][snapshot] = sequence[step]
            else:
                outs[peer * snapshots + snapshot][...] = sequence[step]


def lstm(places, pieces, weight, bias, snapshots, stacked_in, stacked_out):
    groups = places.shape[1]
    count, width = pieces[0].shape[-2:]
    single = jax.ShapeDtypeStruct((count, width), BF16)
    double = jax.ShapeDtypeStruct((snapshots, count, width), BF16)
    outs = [double] * groups if stacked_out else [single] * (groups * snapshots)
    return pl.pallas_call(
        functools.partial(lstm_kernel, groups, snapshots, stacked_in, stacked_out),
        out_shape=outs,
        in_specs=[SMEM] + [VMEM] * (len(pieces) + 2),
        out_specs=[VMEM] * len(outs),
        scratch_shapes=[
            pltpu.VMEM((groups * snapshots, count, width), BF16),
            pltpu.VMEM((count, width), BF16),
            pltpu.VMEM((count, width), F32),
            pltpu.VMEM((count, width), BF16),
            pltpu.VMEM((count, width), F32),
        ],
        compiler_params=params(32),
        name="lstm",
    )(places, *pieces, weight, bias)


def prepare_kernel(groups, places, lists, *refs):
    pieces = refs[: 2 * groups]
    weight, extended, low, high = refs[2 * groups :]
    half, width = pieces[1].shape
    for peer in range(groups):
        base = places[1, peer] * (2 * half)
        for chunk in range(2):
            project_into(pieces[2 * peer + chunk], weight, extended, base + chunk * half)
    bound = low.shape[0] // BS
    for entry in range(2 * bound):
        side, slot = divmod(entry, bound)
        source = pl.multiple_of(lists[entry] * BS, BS)
        (high if side else low)[pl.ds(slot * BS, BS), :] = extended[pl.ds(source, BS), :]


def prepare(snapshot, places, own_list, pieces, weight):
    groups = places.shape[1]
    half, width = pieces[1].shape
    bound = own_list.shape[0] // 2
    own = 2 * half * groups
    specs = [at_snapshot(snapshot, (half, width)), whole((half, width))] * groups
    shapes = [(own, width), (bound * BS, width), (bound * BS, width)]
    return pl.pallas_call(
        functools.partial(prepare_kernel, groups),
        grid=(1,),
        out_shape=[jax.ShapeDtypeStruct(shape, BF16) for shape in shapes],
        in_specs=[SMEM, SMEM] + specs + [whole((width, width))],
        out_specs=[whole(shape) for shape in shapes],
        compiler_params=params(32),
        name="prepare",
    )(places, own_list, *pieces, weight)


def second_kernel(snapshot, parts, rows, cols, field, low, high, vals, *refs):
    out, buffer, extended, total, sem, load_sem = refs[-6:]
    start_tiles(snapshot, vals, sem, buffer, parts)
    side = low.shape[0]
    own = field.shape[0]
    copies = []
    for index, (source, base) in enumerate(((low, 0), (field, side), (high, side + own))):
        copies.append(
            pltpu.make_async_copy(
                source, extended.at[pl.ds(base, source.shape[0])], load_sem.at[index]
            )
        )
    for copy in copies:
        copy.start()
    for copy in copies:
        copy.wait()
    add_tiles(snapshot, rows, cols, vals, sem, buffer, extended, total, parts)
    out[...] = total[...].astype(BF16)


def second(snapshot, rows, cols, field, low, high, vals, before):
    snapshots, tiles = vals.shape[:2]
    own, width = field.shape
    side = low.shape[0]
    parts = 4 if tiles % 4 == 0 else 1
    return pl.pallas_call(
        functools.partial(second_kernel, snapshot, parts),
        grid=(1,),
        out_shape=jax.ShapeDtypeStruct((snapshots, own, width), BF16),
        in_specs=[SMEM, SMEM, ANY, ANY, ANY, ANY] + [ANY] * len(before),
        out_specs=at_snapshot(snapshot, (own, width)),
        scratch_shapes=[
            pltpu.VMEM((tiles, BS, BS), BF16),
            pltpu.VMEM((own + 2 * side, width), BF16),
            pltpu.VMEM((own, width), F32),
            pltpu.SemaphoreType.DMA((parts,)),
            pltpu.SemaphoreType.DMA((3,)),
        ],
        input_output_aliases={6: 0} if before else {},
        compiler_params=params(32),
        name="second",
    )(rows, cols, field, low, high, vals, *before)


def neighbours(low, high):
    count = lax.axis_size("vert")
    forward = [(i, (i + 1) % count) for i in range(count)]
    backward = [(target, source) for source, target in forward]
    return lax.ppermute(high, "vert", forward), lax.ppermute(low, "vert", backward)


def partner(index, step, groups):
    if groups & (groups - 1):
        return (index + step) % groups, (index - step) % groups
    return index ^ step, index ^ step


def exchange(piece, step):
    groups = lax.axis_size("snap")
    if step == 0:
        return piece
    pairs = [(i, partner(i, step, groups)[0]) for i in range(groups)]
    return lax.ppermute(piece, "snap", pairs)


def shards(
    features,
    tile_rows,
    tile_cols,
    tile_vals,
    send_lists,
    conv1_weight,
    conv2_weight,
    lstm_weight,
    lstm_bias,
):
    snapshots = features.shape[0]
    groups = lax.axis_size("snap")
    own_list = lax.dynamic_index_in_dim(send_lists, lax.axis_index("vert"), 0, keepdims=False)
    places = jnp.stack(
        partner(lax.axis_index("snap"), jnp.arange(groups, dtype=jnp.int32), groups)
    ).astype(jnp.int32)
    packed = pick(features, own_list)
    halos = [neighbours(packed[2 * s], packed[2 * s + 1]) for s in range(snapshots)]
    early = []
    before = []
    for s in range(snapshots):
        outs = first(
            s, places, tile_rows, tile_cols, features, *halos[s], conv1_weight, tile_vals, before
        )
        early.append([exchange(outs[2 * peer], peer) for peer in range(groups)])
        before = [outs[2 * peer + 1] for peer in range(groups)]
    late = [exchange(before[peer], peer) for peer in range(groups)]
    pieces = [early[s][peer] for peer in range(groups) for s in range(snapshots)]
    done = lstm(places, pieces, lstm_weight, lstm_bias, snapshots, False, True)
    head = [exchange(done[peer], peer) for peer in range(groups)]
    done = lstm(places, late, lstm_weight, lstm_bias, snapshots, True, False)
    result = []
    for s in range(snapshots):
        tail = [exchange(done[peer * snapshots + s], peer) for peer in range(groups)]
        pieces = [item for pair in zip(head, tail) for item in pair]
        field, low, high = prepare(s, places, own_list, pieces, conv2_weight)
        low, high = neighbours(low, high)
        result = [second(s, tile_rows, tile_cols, field, low, high, tile_vals, result)]
    return result[0]


def solution(mesh):
    placed = (
        P("snap", "vert", None),
        P("snap", "vert"),
        P("snap", "vert"),
        P("snap", "vert", None, None),
        P(),
        P(),
        P(),
        P(),
        P(),
    )
    return jax.shard_map(
        shards, mesh=mesh, in_specs=placed, out_specs=P("snap", "vert", None), check_vma=False
    )
```

```python
import functools

import jax
import jax.numpy as jnp
from jax import lax
from jax.experimental import pallas as pl
from jax.experimental.pallas import tpu as pltpu
from jax.sharding import PartitionSpec as P


BS = 128
GROUP = 8
HBM = pl.BlockSpec(memory_space=pltpu.HBM)
VMEM = pl.BlockSpec(memory_space=pltpu.VMEM)
SMEM = pl.BlockSpec(memory_space=pltpu.SMEM)
BF16 = jnp.bfloat16
F32 = jnp.float32


def params(mib):
    return pltpu.CompilerParams(vmem_limit_bytes=mib << 20)


def block(index):
    return pl.ds(pl.multiple_of(index * BS, BS), BS)


def partner(index, step, groups):
    if groups & (groups - 1):
        return (index + step) % groups, (index - step) % groups
    return index ^ step, index ^ step


def list_halo(snapshot, rows, cols, bound, blocks, table):
    tiles = rows.shape[1]

    def body(tile, found):
        col = cols[snapshot, tile]
        low = col < bound
        high = col >= bound + blocks
        table[0, found] = tile
        table[1, found] = rows[snapshot, tile]
        table[2, found] = jnp.where(low, col, col - blocks)
        return found + jnp.logical_or(low, high).astype(jnp.int32)

    found = lax.fori_loop(0, tiles, body, jnp.int32(0))
    for pad in range(GROUP):
        table[0, found + pad] = 0
        table[1, found + pad] = 0
        table[2, found + pad] = 2 * bound
    table[3, 0] = found


def table_of(tiles):
    return jax.ShapeDtypeStruct((4, tiles + GROUP), jnp.int32)


def pick_kernel(bound, blocks, lists, rows, cols, field, weight, *refs):
    outs = refs[:-4]
    kept, table, sem, weight_sem = refs[-4:]
    device = lax.axis_index("vert")
    copies = [pltpu.make_async_copy(weight, kept, weight_sem)]
    for snapshot in range(len(outs) // 2):
        for entry in range(2 * bound):
            side, slot = divmod(entry, bound)
            copies.append(
                pltpu.make_async_copy(
                    field.at[snapshot, block(lists[device, entry])],
                    outs[2 * snapshot + side].at[block(slot)],
                    sem.at[snapshot, entry],
                )
            )
    for copy in copies:
        copy.start()
    list_halo(0, rows, cols, bound, blocks, table)
    for copy in copies:
        copy.wait()


def pick(features, send_lists, rows, cols, weight):
    snapshots, own, width = features.shape
    bound = send_lists.shape[1] // 2
    side = jax.ShapeDtypeStruct((bound * BS, width), features.dtype)
    operands = (send_lists, rows, cols, features, weight)
    return pl.pallas_call(
        functools.partial(pick_kernel, bound, own // BS),
        out_shape=[side] * (2 * snapshots)
        + [pltpu.VMEM(weight.shape, weight.dtype), table_of(rows.shape[1])],
        in_specs=[SMEM, SMEM, SMEM, HBM, HBM],
        out_specs=[VMEM] * (2 * snapshots) + [VMEM, SMEM],
        scratch_shapes=[
            pltpu.SemaphoreType.DMA((snapshots, 2 * bound)),
            pltpu.SemaphoreType.DMA,
        ],
        compiler_params=params(4),
        cost_estimate=pl.CostEstimate(flops=0, transcendentals=0, bytes_accessed=64 << 20),
        name="pick",
    )(*[pltpu.with_memory_space_constraint(x, pltpu.HBM) for x in operands])


def add_own(snapshot, rows, cols, vals, extended, total, copies=()):
    total[...] = jnp.zeros_like(total)
    tiles = vals.shape[-3]
    each = tiles // max(1, len(copies))
    for tile in range(tiles):
        if copies and tile % each == 0:
            copies[tile // each].wait()
        total[block(rows[snapshot, tile]), :] += jnp.dot(
            vals[0 if copies else snapshot, tile],
            extended[block(cols[snapshot, tile]), :],
            preferred_element_type=F32,
        )


def clear_halo(extended, bound):
    side = bound * BS
    edge = jnp.zeros((side, extended.shape[1]), BF16)
    extended[pl.ds(0, side), :] = edge
    extended[pl.ds(extended.shape[0] - side, side), :] = edge


def first_own_kernel(snapshot, bound, rows, cols, field, weight, vals, total, *refs):
    extended = refs[1]
    own = field.shape[1]
    copies = []
    if snapshot == 0:
        kept, sem = refs[0], refs[2]
        parts = sem.shape[0]
        each = kept.shape[1] // parts
        for part in range(parts):
            span = pl.ds(part * each, each)
            copies.append(pltpu.make_async_copy(vals.at[0, span], kept.at[0, span], sem.at[part]))
            copies[-1].start()
        vals = kept
    clear_halo(extended, bound)
    extended[pl.ds(bound * BS, own), :] = jnp.dot(
        field[snapshot], weight[...], preferred_element_type=F32
    ).astype(BF16)
    if snapshot:
        list_halo(snapshot, rows, cols, bound, own // BS, refs[0])
    add_own(snapshot, rows, cols, vals, extended, total, copies)


def first_own(snapshot, bound, rows, cols, features, weight, vals):
    own, width = features.shape[1:]
    tiles = vals.shape[1]
    parts = 4 if tiles % 4 == 0 else 1
    scratch = [pltpu.VMEM((own + 2 * bound * BS, width), BF16)]
    if snapshot:
        made, made_spec, vals_spec = table_of(tiles), SMEM, VMEM
    else:
        made, made_spec, vals_spec = pltpu.VMEM((1, tiles, BS, BS), BF16), VMEM, HBM
        vals = pltpu.with_memory_space_constraint(vals, pltpu.HBM)
        scratch.append(pltpu.SemaphoreType.DMA((parts,)))
    return pl.pallas_call(
        functools.partial(first_own_kernel, snapshot, bound),
        out_shape=[pltpu.VMEM((own, width), F32), made],
        in_specs=[SMEM, SMEM, VMEM, VMEM, vals_spec],
        out_specs=[VMEM, made_spec],
        scratch_shapes=scratch,
        compiler_params=params(8),
        name="first_own",
    )(rows, cols, features, weight, vals)


def second_own_kernel(snapshot, rows, cols, extended, vals, total):
    add_own(snapshot, rows, cols, vals, extended, total)


def second_own(snapshot, own, rows, cols, extended, vals):
    return pl.pallas_call(
        functools.partial(second_own_kernel, snapshot),
        out_shape=pltpu.VMEM((own, extended.shape[1]), F32),
        in_specs=[SMEM, SMEM, VMEM, VMEM],
        out_specs=VMEM,
        compiler_params=params(8),
        name="second_own",
    )(rows, cols, extended, vals)


def add_halo(snapshot, table, vals, edges, total):
    found = table[3, 0]

    def body(step, carry):
        for inner in range(GROUP):
            entry = step * GROUP + inner
            total[block(table[1, entry]), :] += jnp.dot(
                vals[min(snapshot, vals.shape[0] - 1), table[0, entry]],
                edges[block(table[2, entry]), :],
                preferred_element_type=F32,
            )
        return carry

    lax.fori_loop(0, (found + GROUP - 1) // GROUP, body, 0)


def first_halo_kernel(snapshot, groups, last, table, low, high, weight, vals, partial, *refs):
    earlier = refs[: groups * snapshot] if last else ()
    total, edges = refs[-2:]
    outs = refs[len(earlier) : -2]
    side = low.shape[0]
    edges[pl.ds(0, side), :] = jnp.dot(
        low[...], weight[...], preferred_element_type=F32
    ).astype(BF16)
    edges[pl.ds(side, side), :] = jnp.dot(
        high[...], weight[...], preferred_element_type=F32
    ).astype(BF16)
    edges[pl.ds(2 * side, BS), :] = jnp.zeros((BS, edges.shape[1]), BF16)
    add_halo(snapshot, table, vals, edges, total)
    share = total.shape[0] // groups
    half = share // 2
    rank = lax.axis_index("snap")
    for peer in range(groups):
        base = partner(rank, peer, groups)[0] * share
        for chunk in range(2):
            start = pl.multiple_of(base + chunk * half, half)
            value = jnp.maximum(total[pl.ds(start, half), :], 0.0).astype(BF16)
            if last and chunk:
                for other in range(snapshot):
                    outs[groups + peer][other] = earlier[other * groups + peer][...]
                outs[groups + peer][snapshot] = value
            else:
                outs[chunk * groups + peer][...] = value


def first_halo(snapshot, snapshots, groups, table, low, high, weight, vals, partial, earlier):
    own, width = partial.shape
    last = snapshot + 1 == snapshots
    half = own // groups // 2
    single = jax.ShapeDtypeStruct((half, width), BF16)
    late = jax.ShapeDtypeStruct((snapshots, half, width), BF16) if last else single
    earlier = earlier if last else []
    outs = pl.pallas_call(
        functools.partial(first_halo_kernel, snapshot, groups, last),
        out_shape=[single] * groups + [late] * groups + [pltpu.VMEM((own, width), F32)],
        in_specs=[SMEM] + [VMEM] * (5 + len(earlier)),
        out_specs=[VMEM] * (2 * groups + 1),
        scratch_shapes=[pltpu.VMEM((2 * low.shape[0] + BS, width), BF16)],
        input_output_aliases={5: 2 * groups},
        compiler_params=params(8),
        name="first_halo",
    )(table, low, high, weight, vals, partial, *earlier)
    return outs[:groups], outs[groups : 2 * groups]


def second_halo_kernel(snapshot, table, low, high, vals, partial, *refs):
    out, total, edges, buffer, sem = refs[-5:]
    side = low.shape[0]
    edges[pl.ds(0, side), :] = low[...]
    edges[pl.ds(side, side), :] = high[...]
    edges[pl.ds(2 * side, BS), :] = jnp.zeros((BS, edges.shape[1]), BF16)
    add_halo(snapshot, table, vals, edges, total)
    parts = sem.shape[0]
    each = total.shape[0] // parts
    copies = []
    for part in range(parts):
        rows = pl.ds(part * each, each)
        buffer[rows, :] = total[rows, :].astype(BF16)
        copies.append(
            pltpu.make_async_copy(buffer.at[rows], out.at[snapshot, rows], sem.at[part])
        )
        copies[-1].start()
    for copy in copies:
        copy.wait()


def second_halo(snapshot, table, low, high, vals, partial, before):
    own, width = partial.shape
    snapshots = vals.shape[0]
    aliases = {4: 1}
    if before:
        aliases[5] = 0
    return pl.pallas_call(
        functools.partial(second_halo_kernel, snapshot),
        out_shape=[
            jax.ShapeDtypeStruct((snapshots, own, width), BF16),
            pltpu.VMEM((own, width), F32),
        ],
        in_specs=[SMEM] + [VMEM] * 4 + [HBM] * len(before),
        out_specs=[HBM, VMEM],
        scratch_shapes=[
            pltpu.VMEM((2 * low.shape[0] + BS, width), BF16),
            pltpu.VMEM((own, width), BF16),
            pltpu.SemaphoreType.DMA((4,)),
        ],
        input_output_aliases=aliases,
        compiler_params=params(8),
        name="second_halo",
    )(table, low, high, vals, partial, *before)[0]


def sigmoid(value):
    return 0.5 * jnp.tanh(0.5 * value) + 0.5


def gate_cell(gates, cell, width):
    keep = sigmoid(gates[:, width : 2 * width]) * cell
    cell = keep + sigmoid(gates[:, :width]) * jnp.tanh(gates[:, 2 * width : 3 * width])
    hidden = (sigmoid(gates[:, 3 * width :]) * jnp.tanh(cell)).astype(BF16)
    return hidden, cell


def lstm_kernel(groups, snapshots, stacked_in, stacked_out, *refs):
    ins = refs[: groups if stacked_in else groups * snapshots]
    refs = refs[len(ins) :]
    weight, bias = refs[:2]
    refs = refs[2:]
    outs = refs[: groups if stacked_out else groups * snapshots]
    sequence, hidden0, cell0, hidden1, cell1 = refs[len(outs) :]
    steps, count, width = sequence.shape
    rank = lax.axis_index("snap")
    for peer in range(groups):
        for snapshot in range(snapshots):
            step = partner(rank, peer, groups)[1] * snapshots + snapshot
            if stacked_in:
                sequence[step] = ins[peer][snapshot]
            else:
                sequence[step] = ins[peer * snapshots + snapshot][...]

    def gates(layer, inputs, hidden):
        return (
            jnp.dot(inputs, weight[layer, :width, :], preferred_element_type=F32)
            + jnp.dot(hidden, weight[layer, width:, :], preferred_element_type=F32)
            + bias[layer : layer + 1, :]
        )

    part = count
    pieces = [pl.ds(start, part) for start in range(0, count, part)]
    for ref in (hidden0, cell0, hidden1, cell1):
        ref[...] = jnp.zeros_like(ref)
    for piece in pieces:
        hidden, cell = gate_cell(gates(0, sequence[0, piece], hidden0[piece]), cell0[piece], width)
        hidden0[piece] = hidden
        cell0[piece] = cell

    def both(step, carry):
        for piece in pieces:
            shared = hidden0[piece]
            gates0 = gates(0, sequence[step + 1, piece], shared)
            gates1 = gates(1, shared, hidden1[piece])
            hidden, cell = gate_cell(gates0, cell0[piece], width)
            hidden0[piece] = hidden
            cell0[piece] = cell
            hidden, cell = gate_cell(gates1, cell1[piece], width)
            hidden1[piece] = hidden
            cell1[piece] = cell
            sequence[step, piece] = hidden
        return carry

    lax.fori_loop(0, steps - 1, both, 0)
    for piece in pieces:
        hidden, cell = gate_cell(gates(1, hidden0[piece], hidden1[piece]), cell1[piece], width)
        sequence[steps - 1, piece] = hidden
    for peer in range(groups):
        for snapshot in range(snapshots):
            step = partner(rank, peer, groups)[0] * snapshots + snapshot
            if stacked_out:
                outs[peer][snapshot] = sequence[step]
            else:
                outs[peer * snapshots + snapshot][...] = sequence[step]


def lstm(groups, pieces, weight, bias, snapshots, stacked_in, stacked_out):
    count, width = pieces[0].shape[-2:]
    single = jax.ShapeDtypeStruct((count, width), BF16)
    double = jax.ShapeDtypeStruct((snapshots, count, width), BF16)
    outs = [double] * groups if stacked_out else [single] * (groups * snapshots)
    return pl.pallas_call(
        functools.partial(lstm_kernel, groups, snapshots, stacked_in, stacked_out),
        out_shape=outs,
        in_specs=[VMEM] * (len(pieces) + 2),
        out_specs=[VMEM] * len(outs),
        scratch_shapes=[
            pltpu.VMEM((groups * snapshots, count, width), BF16),
            pltpu.VMEM((count, width), BF16),
            pltpu.VMEM((count, width), F32),
            pltpu.VMEM((count, width), BF16),
            pltpu.VMEM((count, width), F32),
        ],
        compiler_params=params(24),
        name="lstm",
    )(*pieces, weight, bias)


def prepare_kernel(snapshot, groups, lists, *refs):
    rank, device = lax.axis_index("snap"), lax.axis_index("vert")
    pieces = refs[: 2 * groups]
    weight, extended, low, high = refs[2 * groups :]
    half = pieces[1].shape[0]
    side = low.shape[0]
    bound = side // BS
    clear_halo(extended, bound)
    for peer in range(groups):
        base = partner(rank, peer, groups)[1] * (2 * half) + side
        for chunk in range(2):
            piece = pieces[2 * peer + chunk]
            start = pl.multiple_of(base + chunk * half, BS)
            extended[pl.ds(start, half), :] = jnp.dot(
                piece[...] if chunk else piece[snapshot], weight[...], preferred_element_type=F32
            ).astype(BF16)
    for entry in range(2 * bound):
        which, slot = divmod(entry, bound)
        (high if which else low)[block(slot), :] = extended[
            block(lists[device, entry] + bound), :
        ]


def prepare(snapshot, groups, send_lists, pieces, weight):
    half, width = pieces[1].shape
    bound = send_lists.shape[1] // 2
    own = 2 * half * groups
    side = jax.ShapeDtypeStruct((bound * BS, width), BF16)
    return pl.pallas_call(
        functools.partial(prepare_kernel, snapshot, groups),
        out_shape=[pltpu.VMEM((own + 2 * bound * BS, width), BF16), side, side],
        in_specs=[SMEM] + [VMEM] * (2 * groups + 1),
        out_specs=[VMEM] * 3,
        compiler_params=params(8),
        name="prepare",
    )(send_lists, *pieces, weight)


def neighbours(low, high):
    count = lax.axis_size("vert")
    forward = [(i, (i + 1) % count) for i in range(count)]
    backward = [(target, source) for source, target in forward]
    low_edge = lax.ppermute(high, "vert", forward)
    high_edge = lax.ppermute(low, "vert", backward)
    return low_edge, high_edge


def exchange(pieces):
    groups = lax.axis_size("snap")
    received = [pieces[0]]
    for step in range(1, groups):
        pairs = [(i, partner(i, step, groups)[0]) for i in range(groups)]
        received.append(lax.ppermute(pieces[step], "snap", pairs))
    return received


def shards(
    features,
    tile_rows,
    tile_cols,
    tile_vals,
    send_lists,
    conv1_weight,
    conv2_weight,
    lstm_weight,
    lstm_bias,
):
    snapshots, own, _ = features.shape
    groups = lax.axis_size("snap")
    bound = send_lists.shape[1] // 2
    picked = pick(features, send_lists, tile_rows, tile_cols, conv1_weight)
    weight = picked[-2]
    tables = [picked[-1]]
    early, earlier = [], []
    for s in range(snapshots):
        low, high = neighbours(*picked[2 * s : 2 * s + 2])
        partial, made = first_own(s, bound, tile_rows, tile_cols, features, weight, tile_vals)
        if s:
            tables.append(made)
        vals = tile_vals if s else made
        singles, later = first_halo(
            s, snapshots, groups, tables[s], low, high, weight, vals, partial, earlier
        )
        early.append(exchange(singles))
        earlier = earlier + list(later)
    late = exchange(later)
    pieces = [early[s][peer] for peer in range(groups) for s in range(snapshots)]
    done = lstm(groups, pieces, lstm_weight, lstm_bias, snapshots, False, True)
    head = exchange(done)
    done = lstm(groups, late, lstm_weight, lstm_bias, snapshots, True, False)
    result = []
    for s in range(snapshots):
        tail = exchange(done[s::snapshots])
        pieces = [item for pair in zip(head, tail) for item in pair]
        extended, low, high = prepare(s, groups, send_lists, pieces, conv2_weight)
        low, high = neighbours(low, high)
        partial = second_own(s, own, tile_rows, tile_cols, extended, tile_vals)
        result = [second_halo(s, tables[s], low, high, tile_vals, partial, result)]
    return result[0]


def solution(mesh):
    placed = (
        P("snap", "vert", None),
        P("snap", "vert"),
        P("snap", "vert"),
        P("snap", "vert", None, None),
        P(),
        P(),
        P(),
        P(),
        P(),
    )

    def step(*operands):
        mapped = jax.shard_map(
            shards, mesh=mesh, in_specs=placed, out_specs=P("snap", "vert", None), check_vma=False
        )
        return mapped(*operands)

    return step
```
